512 devices in a mesh: band: 16 (over z), owner: 32 (over y, x, core).
Axes of the slice: x: 4, y: 4, z: 16, core: 2. Of those that a mesh axis runs over, the one named last changes fastest.
Arguments:
- user_factors: float32 [262144, 256], P(('band', 'owner')), may hold values from -1.5 to 1.5
- item_factors: float32 [16384, 256], P(('band', 'owner')), may hold values from -1.5 to 1.5
- ratings: bfloat16 [3, 8192, 128, 128], P(None, ('band', 'owner')), may hold values from -6 to 6
- tile_users: int32 [3, 8192], P(None, ('band', 'owner')), may hold values from 0 to 3, as said below
- tile_items: int32 [3, 8192], P(None, ('band', 'owner')), may hold values from 0 to 7, as said below
- tile_count: int32 [3, 512], P(None, ('band', 'owner')), may hold values from 1 to 16, as said below
Outputs:
- user_out: float32 [262144, 256], P(('band', 'owner'))
- item_out: float32 [16384, 256], P(('band', 'owner'))
The draws below stay inside these ranges and needn't reach their ends.
Inputs may be any that keep to these rules, and one draw needn't show every extreme that they name: `tile_users`: within one device and tick, the slots name distinct tiles (user row, item column). `tile_items`: paired with tile_users: the slots of one device and tick name distinct tiles. `tile_count`: each value is 16, 8 or 4, at least 1; in every tick some device has 16.
All inputs are finite; a program needn't handle non-finite values.
Results may differ from the reference program's by a relative error of at most 0.0003.
Values sent between devices are 32-bit elements; how exact they have to be, the bound alone decides.
No kernel may reach another device: no remote copies, remote signals or barrier semaphores. Data moves between devices by JAX's collectives and lax.ppermute only.
A program may use at most 64 MiB of HBM per device.

```python
import jax
import jax.numpy as jnp
from jax import lax

R = 256
P_SIZE = 1024
TILE = 128
TICKS = 3
U_DEV = 512
K_MAX = 16
USERS = 262144
ITEMS = 16384
SLOTS = 8192
N_BAND = 16
N_OWNER = 32


def tile_cells(key):
    base = jax.random.fold_in(key, 7)
    cells = U_DEV // TILE * (P_SIZE // TILE)
    groups = SLOTS // K_MAX
    subkeys = jax.random.split(base, TICKS * groups)

    def pick_cells(subkey):
        return jax.random.permutation(subkey, cells)[:K_MAX]
    chosen = jax.vmap(pick_cells)(subkeys)
    return chosen.reshape(TICKS, SLOTS).astype(jnp.int32)


def draw_tile_users(key, part):
    return (tile_cells(key) // (P_SIZE // TILE)).astype(jnp.int32)


def draw_tile_items(key, part):
    return (tile_cells(key) % (P_SIZE // TILE)).astype(jnp.int32)


def draw_tile_count(key, part):
    groups = SLOTS // K_MAX
    first_key, second_key = jax.random.split(jax.random.fold_in(key, 11))
    powers = jax.random.randint(first_key, (TICKS, groups), 0, 3)
    filled = jnp.where(powers == 0, K_MAX, jnp.where(powers == 1, K_MAX // 2, K_MAX // 4))
    filled = jnp.maximum(filled, 1)
    places = jax.random.randint(second_key, (TICKS,), 0, groups)
    filled = filled.at[jnp.arange(TICKS), places].set(K_MAX)
    return filled.astype(jnp.int32)


def steps_of(key, dims, shards, least, high):
    gain, own = 1.0, jax.random.fold_in(key, 6)
    for axis_at, shards_of in shards:
        steps = jnp.exp(jax.random.uniform(jax.random.fold_in(own, axis_at), (shards_of,), jnp.float32, least / len(shards), high / len(shards)))
        gain = gain * jnp.repeat(steps, dims[axis_at] // shards_of).reshape([-1 if axis == axis_at else 1 for axis in range(len(dims))])
    return gain


def scatter_about(own_key, extent, width, bound, pieces=(), kind=jnp.bfloat16):
    drawn = width * jax.random.normal(own_key, extent, jnp.float32)
    if pieces:
        drawn = drawn * steps_of(own_key, extent, pieces, -0.22, 0.18)
    return jnp.clip(drawn, -bound, bound).astype(kind)


def setup_inputs(seed: int = 0) -> dict:
    keys = jax.random.split(jax.random.key(seed), 7)
    user_factors = scatter_about(keys[0], (USERS, R), 0.25, 1.5, ((0, 512),), jnp.float32)
    item_factors = scatter_about(keys[1], (ITEMS, R), 0.25, 1.5, ((0, 512),), jnp.float32)
    ratings = scatter_about(keys[2], (TICKS, SLOTS, TILE, TILE), 1.0, 6.0, ((1, 512),))
    tile_users = draw_tile_users(jax.random.fold_in(keys[6], 71), 0)
    tile_items = draw_tile_items(jax.random.fold_in(keys[6], 71), 0)
    tile_count = draw_tile_count(jax.random.fold_in(keys[6], 71), 0)
    return dict(user_factors=user_factors, item_factors=item_factors, ratings=ratings, tile_users=tile_users, tile_items=tile_items, tile_count=tile_count)


user_rate = 0.02
item_rate = 0.005
shrink_rate = 0.05
highest = lax.Precision.HIGHEST


def slot_update(user_block, item_panel, rating_tiles, tile_rows, tile_cols, filled):
    user_tiles = user_block[tile_rows]
    item_tiles = item_panel[tile_cols]
    active = (jnp.arange(K_MAX) < filled).astype(jnp.float32)
    predicted = jnp.einsum("kur,kir->kui", user_tiles, item_tiles, precision=highest)
    errors = (rating_tiles.astype(jnp.float32) - predicted) * active[:, None, None]
    user_grads = jnp.einsum("kui,kir->kur", errors, item_tiles, precision=highest)
    item_grads = jnp.einsum("kui,kur->kir", errors, user_tiles, precision=highest)
    user_hot = (tile_rows[:, None] == jnp.arange(user_block.shape[0])[None, :]).astype(jnp.float32)
    item_hot = (tile_cols[:, None] == jnp.arange(item_panel.shape[0])[None, :]).astype(jnp.float32)
    user_sum = jnp.einsum("kt,kur->tur", user_hot, user_grads, precision=highest)
    item_sum = jnp.einsum("kt,kir->tir", item_hot, item_grads, precision=highest)
    new_users = user_block * (1.0 - user_rate * shrink_rate) + user_rate * user_sum
    return new_users, item_sum


def reference(user_factors, item_factors, ratings, tile_users, tile_items, tile_count):
    bands = N_BAND
    owners = N_OWNER
    user_blocks = user_factors.reshape(bands, owners, U_DEV // TILE, TILE, R)
    panels_all = item_factors.reshape(bands, P_SIZE // TILE, TILE, R)
    for tick_index in range(TICKS):
        rating_tiles = ratings[tick_index].reshape(bands, owners, K_MAX, TILE, TILE)
        tile_rows = tile_users[tick_index].reshape(bands, owners, K_MAX)
        tile_cols = tile_items[tick_index].reshape(bands, owners, K_MAX)
        filled = tile_count[tick_index].reshape(bands, owners)
        current = jnp.roll(panels_all, -tick_index, axis=0)

        def band_step(operands):
            block, item_panel, tiles_here, rows_here, cols_here, filled_here = operands
            new_users, item_sums = jax.vmap(slot_update, in_axes=(0, None, 0, 0, 0, 0))(
                block, item_panel, tiles_here, rows_here, cols_here, filled_here)
            new_panel = item_panel * (1.0 - item_rate * shrink_rate) + item_rate * jnp.sum(item_sums, axis=0)
            return new_users, new_panel

        user_blocks, current = lax.map(band_step, (user_blocks, current, rating_tiles, tile_rows, tile_cols, filled))
        panels_all = jnp.roll(current, tick_index, axis=0)
    final_panels = jnp.roll(panels_all, -(TICKS - 1), axis=0)
    return user_blocks.reshape(-1, R), final_panels.reshape(-1, R)
```

```python
import functools

import jax
import jax.numpy as jnp
from jax import lax
from jax.experimental import pallas as pl
from jax.experimental.pallas import tpu as pltpu
from jax.sharding import PartitionSpec as P

R = 256
P_SIZE = 1024
TILE = 128
HALF = TILE // 2
TICKS = 3
K_MAX = 16
U_DEV = 512
U_TILES = U_DEV // TILE
I_TILES = P_SIZE // TILE
ITEMS_CORE = P_SIZE // 2
CHIPS = 16
SHARE = 32
CELLS = U_TILES * I_TILES

user_rate = 0.02
item_rate = 0.005
shrink_rate = 0.05
bf16 = jnp.bfloat16
f32 = jnp.float32

SAME_CORE = [[2 * chip + core for chip in range(CHIPS)] for core in range(2)]
PARTNERS = [(i, i ^ 1) for i in range(2 * CHIPS)]


def halves(x):
    top = x.astype(bf16)
    return top, (x - top.astype(f32)).astype(bf16)


def dot3(a, b, dims):
    (a_top, a_low), (b_top, b_low) = a, b
    dot = lambda x, y: lax.dot_general(x, y, (dims, ((), ())), preferred_element_type=f32)
    return dot(a_top, b_top) + (dot(a_top, b_low) + dot(a_low, b_top))


VMEM = pl.BlockSpec(memory_space=pltpu.VMEM)
ANY = pl.BlockSpec(memory_space=pl.ANY)
SMEM = pl.BlockSpec(memory_space=pltpu.SMEM)
WIDTH = 2 * TILE
BLOCKS = 2 * U_DEV // WIDTH


def shape(dims, dtype):
    return jax.ShapeDtypeStruct(dims, dtype)


def call(kernel, outs, in_specs, out_specs, scratch, flops, nbytes, grant=60 * 1024):
    return pl.pallas_call(
        kernel,
        out_shape=outs,
        in_specs=in_specs,
        out_specs=out_specs,
        scratch_shapes=scratch,
        compiler_params=pltpu.CompilerParams(vmem_limit_bytes=grant * 1024),
        cost_estimate=pl.CostEstimate(flops=flops, bytes_accessed=nbytes, transcendentals=0),
    )


def turn_kernel(tick, core_ref, map_ref, tiles_hbm, kept_hbm, sent_hbm, tiles, kept, sent, turned, sems):
    core = core_ref[0]
    group = K_MAX // 4

    def fetch(g):
        slots = pl.ds(g * group, group)
        return pltpu.make_async_copy(tiles_hbm.at[tick, slots], tiles.at[slots], sems.at[g])

    def put(g, which):
        buf, hbm = ((kept, kept_hbm), (sent, sent_hbm))[which]
        slots = pl.ds(g * group, group)
        return pltpu.make_async_copy(buf.at[slots], hbm.at[slots], sems.at[4 + 2 * g + which])

    for g in range(4):
        fetch(g).start()
    lane = lax.broadcasted_iota(jnp.int32, (8, TILE), 1)
    row = jnp.zeros((8, TILE), jnp.int32)
    for cell in range(CELLS):
        row = jnp.where(lane == cell, map_ref[tick * CELLS + cell], row)
    sent[K_MAX, pl.ds(0, 8), :] = row.astype(f32)
    sent[K_MAX, pl.ds(8, HALF - 8), :] = jnp.zeros((HALF - 8, TILE), f32)
    last = pltpu.make_async_copy(sent.at[pl.ds(K_MAX, 1)], sent_hbm.at[pl.ds(K_MAX, 1)], sems.at[12])
    last.start()
    for g in range(4):
        fetch(g).wait()
        for k in range(g * group, (g + 1) * group):
            turned[k] = tiles[k].astype(f32).T
            for part in range(2):
                rows = pl.ds(part * SHARE, SHARE)
                mine = pl.multiple_of(part * HALF + core * SHARE, SHARE)
                theirs = pl.multiple_of(part * HALF + (1 - core) * SHARE, SHARE)
                kept[k, rows, :] = turned[k, pl.ds(mine, SHARE), :]
                sent[k, rows, :] = turned[k, pl.ds(theirs, SHARE), :]
        put(g, 0).start()
        put(g, 1).start()
    for g in range(4):
        put(g, 0).wait()
        put(g, 1).wait()
    last.wait()


def turned_tiles(tick, core, slot_map, ratings):
    return call(
        functools.partial(turn_kernel, tick),
        (shape((K_MAX, HALF, TILE), f32), shape((K_MAX + 1, HALF, TILE), f32)),
        [SMEM, SMEM, ANY], (ANY, ANY),
        [pltpu.VMEM((K_MAX, TILE, TILE), bf16), pltpu.VMEM((K_MAX, HALF, TILE), f32),
         pltpu.VMEM((K_MAX + 1, HALF, TILE), f32), pltpu.VMEM((K_MAX, TILE, TILE), f32),
         pltpu.SemaphoreType.DMA((13,))],
        1000000, 1600000,
    )(core, slot_map, ratings)


def split_kernel(own_ref, other_ref, top_ref, low_ref):
    for part, ref in enumerate((own_ref, other_ref)):
        rows = pl.ds(part * U_DEV, U_DEV)
        top_ref[rows, :], low_ref[rows, :] = halves(ref[...])


def split_users(own, other):
    out = shape((2 * U_DEV, R), bf16)
    return call(split_kernel, (out, out), [VMEM] * 2, (VMEM,) * 2, [], 1000000, 2000000)(own, other)


def error_kernel(own_map, other_map, panel_hbm, top_hbm, low_hbm, own_hbm, other_hbm,
                 grad_hbm, err_top_hbm, err_low_hbm,
                 panel_ref, top_ref, low_ref, own_tiles, other_tiles, predicted, err_top, err_low, grad_ref, sems):
    def rows(block):
        return pl.ds(block * WIDTH, WIDTH)

    loads = [pltpu.make_async_copy(panel_hbm, panel_ref, sems.at[0])]
    for block in range(BLOCKS):
        loads.append(pltpu.make_async_copy(top_hbm.at[rows(block)], top_ref.at[rows(block)], sems.at[1 + 2 * block]))
        loads.append(pltpu.make_async_copy(low_hbm.at[rows(block)], low_ref.at[rows(block)], sems.at[2 + 2 * block]))
    first = 1 + 2 * BLOCKS
    loads.append(pltpu.make_async_copy(own_hbm, own_tiles, sems.at[first]))
    loads.append(pltpu.make_async_copy(other_hbm.at[pl.ds(0, K_MAX)], other_tiles, sems.at[first + 1]))
    for copy in [*loads[:5], loads[first], *loads[5:first], loads[first + 1]]:
        copy.start()

    def put(block, which):
        source, into = ((err_top, err_top_hbm), (err_low, err_low_hbm))[which]
        return pltpu.make_async_copy(source.at[block], into.at[block], sems.at[first + 2 + 2 * block + which])

    def send(part):
        cut = pl.ds(part * TILE, TILE)
        return pltpu.make_async_copy(grad_ref.at[cut], grad_hbm.at[cut], sems.at[first + 2 + 2 * BLOCKS + part])

    loads[0].wait()
    panel = halves(panel_ref[...])

    def users(block):
        return top_ref[rows(block), :], low_ref[rows(block), :]

    def predict(block):
        loads[1 + 2 * block].wait()
        loads[2 + 2 * block].wait()
        predicted[block] = dot3(panel, users(block), ((1,), (1,)))

    predict(0)
    for block in range(BLOCKS):
        if block + 1 < BLOCKS:
            predict(block + 1)
        mine = block * WIDTH < U_DEV
        slot_map, tiles = (own_map, own_tiles) if mine else (other_map, other_tiles)
        if block * WIDTH % U_DEV == 0:
            loads[first if mine else first + 1].wait()
        for item in range(I_TILES):
            cut = pl.ds(item * HALF, HALF)
            for part in range(2):
                user = (block * 2 + part) % U_TILES
                slot = slot_map[user * I_TILES + item]
                lanes = pl.ds(part * TILE, TILE)
                error = tiles[jnp.maximum(slot, 0)] - predicted[block, cut, lanes]
                error = jnp.where(slot >= 0, error, 0.0)
                err_top[block, cut, lanes], err_low[block, cut, lanes] = halves(error)
        put(block, 0).start()
        put(block, 1).start()
        if block == 0:
            grad_ref[...] = dot3((err_top[block], err_low[block]), users(block), ((1,), (0,)))
        elif block + 1 < BLOCKS:
            grad_ref[...] += dot3((err_top[block], err_low[block]), users(block), ((1,), (0,)))
        else:
            for part in range(ITEMS_CORE // TILE):
                cut = pl.ds(part * TILE, TILE)
                grad_ref[cut, :] += dot3((err_top[block, cut, :], err_low[block, cut, :]), users(block), ((1,), (0,)))
                send(part).start()
    for block in range(BLOCKS):
        put(block, 0).wait()
        put(block, 1).wait()
    for part in range(ITEMS_CORE // TILE):
        send(part).wait()


def errors_and_item_grad(own_map, other_map, panel, top, low, own_tiles, other_tiles):
    err = (BLOCKS, ITEMS_CORE, WIDTH)
    tiles = pltpu.VMEM((K_MAX, HALF, TILE), f32)
    panel_shape = pltpu.VMEM((ITEMS_CORE, R), f32)
    user = pltpu.VMEM((2 * U_DEV, R), bf16)
    return call(
        error_kernel,
        (shape((ITEMS_CORE, R), f32), shape(err, bf16), shape(err, bf16)),
        [SMEM] * 2 + [ANY] * 5, (ANY,) * 3,
        [panel_shape, user, user, tiles, tiles, pltpu.VMEM(err, f32), pltpu.VMEM(err, bf16), pltpu.VMEM(err, bf16),
         panel_shape, pltpu.SemaphoreType.DMA((3 + 4 * BLOCKS + ITEMS_CORE // TILE,))],
        1600000000, 6000000, 54000,
    )(own_map, other_map, panel, top, low, own_tiles, other_tiles)


def user_grad_kernel(err_top_hbm, err_low_hbm, panel_hbm, grad_hbm, err_top, err_low, panel_ref, grad, sems):
    def fetch(block, which):
        source, into = ((err_top_hbm, err_top), (err_low_hbm, err_low))[which]
        return pltpu.make_async_copy(source.at[block], into.at[block], sems.at[2 * block + which])

    def put(block):
        rows = pl.ds(block * WIDTH, WIDTH)
        return pltpu.make_async_copy(grad.at[rows], grad_hbm.at[rows], sems.at[2 * BLOCKS + block])

    panel_copy = pltpu.make_async_copy(panel_hbm, panel_ref, sems.at[3 * BLOCKS])
    panel_copy.start()
    for block in range(BLOCKS):
        fetch(block, 0).start()
        fetch(block, 1).start()
    panel_copy.wait()
    panel = halves(panel_ref[...])
    for block in range(BLOCKS):
        fetch(block, 0).wait()
        fetch(block, 1).wait()
        grad[pl.ds(block * WIDTH, WIDTH), :] = dot3((err_top[block], err_low[block]), panel, ((0,), (0,)))
        put(block).start()
    for block in range(BLOCKS):
        put(block).wait()


def user_grads(err_top, err_low, panel):
    err = (BLOCKS, ITEMS_CORE, WIDTH)
    return call(
        user_grad_kernel,
        shape((2 * U_DEV, R), f32), [ANY] * 3, ANY,
        [pltpu.VMEM(err, bf16), pltpu.VMEM(err, bf16), pltpu.VMEM((ITEMS_CORE, R), f32),
         pltpu.VMEM((2 * U_DEV, R), f32), pltpu.SemaphoreType.DMA((3 * BLOCKS + 1,))],
        800000000, 4000000, 54000,
    )(err_top, err_low, panel)


def stepped(user, here, there):
    return user * (1.0 - user_rate * shrink_rate) + user_rate * (here + there)


def update_kernel(own_hbm, other_hbm, here_hbm, there_hbm, own_out, other_out, top_ref, low_ref,
                  user, here, there, sems):
    half = BLOCKS // 2

    def rows(block):
        return pl.ds(block * WIDTH, WIDTH)

    def part(block, own, other):
        return (own if block < half else other).at[rows(block % half)]

    def fetch(block, which):
        source, into = (
            (part(block, own_hbm, other_hbm), user),
            (here_hbm.at[rows(block)], here),
            (there_hbm.at[rows((block + half) % BLOCKS)], there),
        )[which]
        return pltpu.make_async_copy(source, into.at[rows(block)], sems.at[4 * block + which])

    def put(block):
        return pltpu.make_async_copy(user.at[rows(block)], part(block, own_out, other_out), sems.at[4 * block + 3])

    for block in range(BLOCKS):
        for which in range(3):
            fetch(block, which).start()
    for block in range(BLOCKS):
        for which in range(3):
            fetch(block, which).wait()
        new = stepped(user[rows(block), :], here[rows(block), :], there[rows(block), :])
        user[rows(block), :] = new
        put(block).start()
        top_ref[rows(block), :], low_ref[rows(block), :] = halves(new)
    for block in range(BLOCKS):
        put(block).wait()


def updated_users(own, other, here, there):
    out = shape((2 * U_DEV, R), bf16)
    new = shape((U_DEV, R), f32)
    both = pltpu.VMEM((2 * U_DEV, R), f32)
    return call(
        update_kernel, (new, new, out, out), [ANY] * 4, (ANY, ANY, VMEM, VMEM),
        [both, both, both, pltpu.SemaphoreType.DMA((4 * BLOCKS,))], 1000000, 5000000,
    )(own, other, here, there)


def swapped(x):
    return lax.ppermute(x, "owner", PARTNERS)


def exchanged(blocks):
    return lax.all_to_all(blocks, "owner", split_axis=0, concat_axis=0, axis_index_groups=SAME_CORE, tiled=True)


def passed_along(block, axis, distance):
    devices = range(lax.axis_size(axis))
    route = [((i - distance) % len(devices), i) for i in devices]
    return lax.ppermute(block, axis, route)


def slot_maps(tile_users, tile_items, tile_count):
    slots = jnp.arange(K_MAX)[None, :, None]
    cell = (tile_users * I_TILES + tile_items)[:, :, None]
    live = (slots < tile_count[:, :, None]) & (cell == jnp.arange(CELLS)[None, None, :])
    return jnp.max(jnp.where(live, slots, -1), axis=1).astype(jnp.int32)


def shards(user_factors, item_factors, ratings, tile_users, tile_items, tile_count):
    core = lax.rem(lax.axis_index("owner"), 2).reshape(1)
    own, share = user_factors, item_factors
    other = swapped(own)
    own_map = slot_maps(tile_users, tile_items, tile_count)
    top, low = split_users(own, other)
    for tick in range(TICKS):
        kept, sent = turned_tiles(tick, core, own_map.reshape(-1), ratings)
        got = swapped(sent)
        other_map = got[K_MAX, 0, :CELLS].astype(jnp.int32)
        panel = exchanged(jnp.broadcast_to(share[None], (CHIPS, SHARE, R))).reshape(ITEMS_CORE, R)
        item_grad, err_top, err_low = errors_and_item_grad(
            own_map[tick], other_map, panel, top, low, kept, got)
        parts = exchanged(item_grad.reshape(CHIPS, SHARE, R))
        here = user_grads(err_top, err_low, panel)
        if tick + 1 < TICKS:
            there = swapped(here)
            own, other, top, low = updated_users(own, other, here, there)
        else:
            there = swapped(here[U_DEV:])
            own, parts = lax.optimization_barrier((stepped(own, here[:U_DEV], there), parts))
        share = share * (1.0 - item_rate * shrink_rate) + item_rate * parts.sum(axis=0)
        if tick + 1 < TICKS:
            share = passed_along(share, "band", -1)
    return own, share


def solution(mesh):
    placed = (
        P(("band", "owner"), None),
        P(("band", "owner"), None),
        P(None, ("band", "owner"), None, None),
        P(None, ("band", "owner")),
        P(None, ("band", "owner")),
        P(None, ("band", "owner")),
    )
    return jax.shard_map(
        shards,
        mesh=mesh,
        in_specs=placed,
        out_specs=(P(("band", "owner"), None), P(("band", "owner"), None)),
        check_vma=False,
    )
```

```python
import functools

import jax
import jax.numpy as jnp
from jax import lax
from jax.experimental import pallas as pl
from jax.experimental.pallas import tpu as pltpu
from jax.sharding import PartitionSpec as P

R = 256
P_SIZE = 1024
TILE = 128
HALF = TILE // 2
TICKS = 3
K_MAX = 16
U_DEV = 512
U_TILES = U_DEV // TILE
I_TILES = P_SIZE // TILE
ITEMS_CORE = P_SIZE // 2
CHIPS = 16
SHARE = 32
CELLS = U_TILES * I_TILES

user_rate = 0.02
item_rate = 0.005
shrink_rate = 0.05
bf16 = jnp.bfloat16
f32 = jnp.float32

SAME_CORE = [[2 * chip + core for chip in range(CHIPS)] for core in range(2)]
PARTNERS = [(i, i ^ 1) for i in range(2 * CHIPS)]


def halves(x):
    top = x.astype(bf16)
    return top, (x - top.astype(f32)).astype(bf16)


def dot3(a, b, dims):
    (a_top, a_low), (b_top, b_low) = a, b
    dot = lambda x, y: lax.dot_general(x, y, (dims, ((), ())), preferred_element_type=f32)
    return dot(a_top, b_top) + (dot(a_top, b_low) + dot(a_low, b_top))


VMEM = pl.BlockSpec(memory_space=pltpu.VMEM)
ANY = pl.BlockSpec(memory_space=pl.ANY)
SMEM = pl.BlockSpec(memory_space=pltpu.SMEM)
WIDTH = 2 * TILE
BLOCKS = 2 * U_DEV // WIDTH
STEP_GRANT = 53800
UPDATE_GRANT = 60 * 1024


def shape(dims, dtype):
    return jax.ShapeDtypeStruct(dims, dtype)


def call(kernel, outs, in_specs, out_specs, scratch, flops, nbytes, grant=60 * 1024):
    return pl.pallas_call(
        kernel,
        out_shape=outs,
        in_specs=in_specs,
        out_specs=out_specs,
        scratch_shapes=scratch,
        compiler_params=pltpu.CompilerParams(vmem_limit_bytes=grant * 1024),
        cost_estimate=pl.CostEstimate(flops=flops, bytes_accessed=nbytes, transcendentals=0),
    )


def turn_kernel(tick, core_ref, map_ref, tiles_hbm, kept_hbm, sent_hbm, tiles, kept, sent, turned, sems):
    core = core_ref[0]
    group = K_MAX // 4

    def fetch(g):
        slots = pl.ds(g * group, group)
        return pltpu.make_async_copy(tiles_hbm.at[tick, slots], tiles.at[slots], sems.at[g])

    def put(g, which):
        buf, hbm = ((kept, kept_hbm), (sent, sent_hbm))[which]
        slots = pl.ds(g * group, group)
        return pltpu.make_async_copy(buf.at[slots], hbm.at[slots], sems.at[4 + 2 * g + which])

    for g in range(4):
        fetch(g).start()
    lane = lax.broadcasted_iota(jnp.int32, (8, TILE), 1)
    row = jnp.zeros((8, TILE), jnp.int32)
    for cell in range(CELLS):
        row = jnp.where(lane == cell, map_ref[tick * CELLS + cell], row)
    sent[K_MAX, pl.ds(0, 8), :] = row.astype(f32)
    sent[K_MAX, pl.ds(8, HALF - 8), :] = jnp.zeros((HALF - 8, TILE), f32)
    last = pltpu.make_async_copy(sent.at[pl.ds(K_MAX, 1)], sent_hbm.at[pl.ds(K_MAX, 1)], sems.at[12])
    last.start()
    for g in range(4):
        fetch(g).wait()
        for k in range(g * group, (g + 1) * group):
            turned[k] = tiles[k].T
            for part in range(2):
                rows = pl.ds(part * SHARE, SHARE)
                mine = pl.multiple_of(part * HALF + core * SHARE, SHARE)
                theirs = pl.multiple_of(part * HALF + (1 - core) * SHARE, SHARE)
                kept[k, rows, :] = turned[k, pl.ds(mine, SHARE), :]
                sent[k, rows, :] = turned[k, pl.ds(theirs, SHARE), :].astype(f32)
        put(g, 0).start()
        put(g, 1).start()
    for g in range(4):
        put(g, 0).wait()
        put(g, 1).wait()
    last.wait()


def turned_tiles(tick, core, slot_map, ratings):
    tile = pltpu.VMEM((K_MAX, TILE, TILE), bf16)
    return call(
        functools.partial(turn_kernel, tick),
        (shape((K_MAX, HALF, TILE), bf16), shape((K_MAX + 1, HALF, TILE), f32)),
        [SMEM, SMEM, ANY], (ANY, ANY),
        [tile, pltpu.VMEM((K_MAX, HALF, TILE), bf16), pltpu.VMEM((K_MAX + 1, HALF, TILE), f32), tile,
         pltpu.SemaphoreType.DMA((13,))],
        1000000, 1600000,
    )(core, slot_map, ratings)


def step_kernel(own_map, other_map, panel_hbm, own_users, other_users, own_hbm, other_hbm, item_hbm, user_hbm,
                panel_ref, users, own_tiles, other_tiles, predicted, item_grad, user_grad, sems):
    half = BLOCKS // 2
    parts = ITEMS_CORE // TILE

    def rows(block):
        return pl.ds(block * WIDTH, WIDTH)

    panel_load = pltpu.make_async_copy(panel_hbm, panel_ref, sems.at[0])
    own_load = pltpu.make_async_copy(own_hbm, own_tiles, sems.at[1])
    other_load = pltpu.make_async_copy(other_hbm.at[pl.ds(0, K_MAX)], other_tiles, sems.at[2])
    user_loads = [
        pltpu.make_async_copy(
            (own_users if block < half else other_users).at[rows(block % half)], users.at[rows(block)],
            sems.at[3 + block])
        for block in range(BLOCKS)
    ]
    for copy in [panel_load, user_loads[0], own_load, *user_loads[1:], other_load]:
        copy.start()

    def send_items(part):
        cut = pl.ds(part * TILE, TILE)
        return pltpu.make_async_copy(item_grad.at[cut], item_hbm.at[cut], sems.at[3 + BLOCKS + part])

    def send_users(block):
        return pltpu.make_async_copy(
            user_grad.at[rows(block)], user_hbm.at[rows(block)], sems.at[3 + BLOCKS + parts + block])

    panel_load.wait()
    panel = halves(panel_ref[...])

    def predict(block):
        user_loads[block].wait()
        split = halves(users[rows(block), :])
        predicted[block] = dot3(panel, split, ((1,), (1,)))
        return split

    split = predict(0)
    for block in range(BLOCKS):
        after = predict(block + 1) if block + 1 < BLOCKS else None
        slot_map, tiles = (own_map, own_tiles) if block < half else (other_map, other_tiles)
        if block % half == 0:
            (own_load if block < half else other_load).wait()
        tops, lows = [], []
        for item in range(I_TILES):
            cut = pl.ds(item * HALF, HALF)
            errors = []
            for part in range(2):
                slot = slot_map[(block * 2 + part) % U_TILES * I_TILES + item]
                error = tiles[jnp.maximum(slot, 0)].astype(f32) - predicted[block, cut, pl.ds(part * TILE, TILE)]
                errors.append(jnp.where(slot >= 0, error, 0.0))
            top, low = halves(jnp.concatenate(errors, axis=1))
            tops.append(top)
            lows.append(low)
        error = jnp.concatenate(tops, axis=0), jnp.concatenate(lows, axis=0)
        user_grad[rows(block), :] = dot3(error, panel, ((0,), (0,)))
        send_users(block).start()
        if block == 0:
            item_grad[...] = dot3(error, split, ((1,), (0,)))
        elif block + 1 < BLOCKS:
            item_grad[...] += dot3(error, split, ((1,), (0,)))
        else:
            for part in range(parts):
                cut = slice(part * TILE, (part + 1) * TILE)
                item_grad[cut, :] += dot3((error[0][cut], error[1][cut]), split, ((1,), (0,)))
                send_items(part).start()
        split = after
    for block in range(BLOCKS):
        send_users(block).wait()
    for part in range(parts):
        send_items(part).wait()


def item_and_user_grads(own_map, other_map, panel, own, other, own_tiles, other_tiles):
    half_panel = pltpu.VMEM((ITEMS_CORE, R), f32)
    both = pltpu.VMEM((2 * U_DEV, R), f32)
    cut = (K_MAX, HALF, TILE)
    return call(
        step_kernel,
        (shape((ITEMS_CORE, R), f32), shape((2 * U_DEV, R), f32)),
        [SMEM] * 2 + [ANY] * 5, (ANY,) * 2,
        [half_panel, both, pltpu.VMEM(cut, bf16), pltpu.VMEM(cut, f32),
         pltpu.VMEM((BLOCKS, ITEMS_CORE, WIDTH), f32), half_panel, both,
         pltpu.SemaphoreType.DMA((3 + 2 * BLOCKS + ITEMS_CORE // TILE,))],
        2400000000, 4000000, STEP_GRANT,
    )(own_map, other_map, panel, own, other, own_tiles, other_tiles)


def stepped(user, here, there):
    return user * (1.0 - user_rate * shrink_rate) + user_rate * (here + there)


def update_kernel(own_hbm, other_hbm, here_hbm, there_hbm, own_out, other_out, user, here, there, sems):
    half = BLOCKS // 2

    def rows(block):
        return pl.ds(block * WIDTH, WIDTH)

    def part(block, own, other):
        return (own if block < half else other).at[rows(block % half)]

    def fetch(block, which):
        source, into = (
            (part(block, own_hbm, other_hbm), user),
            (here_hbm.at[rows(block)], here),
            (there_hbm.at[rows((block + half) % BLOCKS)], there),
        )[which]
        return pltpu.make_async_copy(source, into.at[rows(block)], sems.at[4 * block + which])

    def put(block):
        return pltpu.make_async_copy(user.at[rows(block)], part(block, own_out, other_out), sems.at[4 * block + 3])

    for block in range(BLOCKS):
        for which in range(3):
            fetch(block, which).start()
    for block in range(BLOCKS):
        for which in range(3):
            fetch(block, which).wait()
        user[rows(block), :] = stepped(user[rows(block), :], here[rows(block), :], there[rows(block), :])
        put(block).start()
    for block in range(BLOCKS):
        put(block).wait()


def updated_users(own, other, here, there):
    new = shape((U_DEV, R), f32)
    both = pltpu.VMEM((2 * U_DEV, R), f32)
    return call(
        update_kernel, (new, new), [ANY] * 4, (ANY, ANY),
        [both, both, both, pltpu.SemaphoreType.DMA((4 * BLOCKS,))], 1000000, 4000000, UPDATE_GRANT,
    )(own, other, here, there)


def swapped(x):
    return lax.ppermute(x, "owner", PARTNERS)


def exchanged(blocks):
    return lax.all_to_all(blocks, "owner", split_axis=0, concat_axis=0, axis_index_groups=SAME_CORE, tiled=True)


def passed_along(block, axis, distance):
    devices = range(lax.axis_size(axis))
    route = [((i - distance) % len(devices), i) for i in devices]
    return lax.ppermute(block, axis, route)


def slot_maps(tile_users, tile_items, tile_count):
    slots = jnp.arange(K_MAX)[None, :, None]
    cell = (tile_users * I_TILES + tile_items)[:, :, None]
    live = (slots < tile_count[:, :, None]) & (cell == jnp.arange(CELLS)[None, None, :])
    return jnp.max(jnp.where(live, slots, -1), axis=1).astype(jnp.int32)


def shards(user_factors, item_factors, ratings, tile_users, tile_items, tile_count):
    core = lax.rem(lax.axis_index("owner"), 2).reshape(1)
    own, share = user_factors, item_factors
    other = swapped(own)
    own_map = slot_maps(tile_users, tile_items, tile_count)
    for tick in range(TICKS):
        kept, sent = turned_tiles(tick, core, own_map.reshape(-1), ratings)
        got = swapped(sent)
        other_map = got[K_MAX, 0, :CELLS].astype(jnp.int32)
        panel = exchanged(jnp.broadcast_to(share[None], (CHIPS, SHARE, R))).reshape(ITEMS_CORE, R)
        item_grad, here = item_and_user_grads(own_map[tick], other_map, panel, own, other, kept, got)
        parts = exchanged(item_grad.reshape(CHIPS, SHARE, R))
        if tick + 1 < TICKS:
            there = swapped(here)
            own, other = updated_users(own, other, here, there)
        else:
            there = swapped(here[U_DEV:])
            own, parts = lax.optimization_barrier((stepped(own, here[:U_DEV], there), parts))
        share = share * (1.0 - item_rate * shrink_rate) + item_rate * parts.sum(axis=0)
        if tick + 1 < TICKS:
            share = passed_along(share, "band", -1)
    return own, share


def solution(mesh):
    placed = (
        P(("band", "owner"), None),
        P(("band", "owner"), None),
        P(None, ("band", "owner"), None, None),
        P(None, ("band", "owner")),
        P(None, ("band", "owner")),
        P(None, ("band", "owner")),
    )
    return jax.shard_map(
        shards,
        mesh=mesh,
        in_specs=placed,
        out_specs=(P(("band", "owner"), None), P(("band", "owner"), None)),
        check_vma=False,
    )
```

```python
import functools

import jax
import jax.numpy as jnp
from jax import lax
from jax.experimental import pallas as pl
from jax.experimental.pallas import tpu as pltpu
from jax.sharding import PartitionSpec as P

R = 256
P_SIZE = 1024
TILE = 128
HALF = TILE // 2
TICKS = 3
K_MAX = 16
U_DEV = 512
U_TILES = U_DEV // TILE
I_TILES = P_SIZE // TILE
ITEMS_CORE = P_SIZE // 2
CHIPS = 16
SHARE = 32
CELLS = U_TILES * I_TILES

user_rate = 0.02
item_rate = 0.005
shrink_rate = 0.05
bf16 = jnp.bfloat16
f32 = jnp.float32

SAME_CORE = [[2 * chip + core for chip in range(CHIPS)] for core in range(2)]
PARTNERS = [(i, i ^ 1) for i in range(2 * CHIPS)]


def halves(x):
    top = x.astype(bf16)
    return top, (x - top.astype(f32)).astype(bf16)


def dot3(a, b, dims):
    (a_top, a_low), (b_top, b_low) = a, b
    dot = lambda x, y: lax.dot_general(x, y, (dims, ((), ())), preferred_element_type=f32)
    return dot(a_top, b_top) + (dot(a_top, b_low) + dot(a_low, b_top))


VMEM = pl.BlockSpec(memory_space=pltpu.VMEM)
ANY = pl.BlockSpec(memory_space=pl.ANY)
SMEM = pl.BlockSpec(memory_space=pltpu.SMEM)
WIDTH = 2 * TILE
BLOCKS = 2 * U_DEV // WIDTH
STEP_GRANT = 54000
UPDATE_GRANT = 60 * 1024


def shape(dims, dtype):
    return jax.ShapeDtypeStruct(dims, dtype)


def call(kernel, outs, in_specs, out_specs, scratch, flops, nbytes, grant=60 * 1024):
    return pl.pallas_call(
        kernel,
        out_shape=outs,
        in_specs=in_specs,
        out_specs=out_specs,
        scratch_shapes=scratch,
        compiler_params=pltpu.CompilerParams(vmem_limit_bytes=grant * 1024),
        cost_estimate=pl.CostEstimate(flops=flops, bytes_accessed=nbytes, transcendentals=0),
    )


def turn_kernel(tick, core_ref, rows_ref, cols_ref, count_ref, tiles_hbm, kept_hbm, sent_hbm,
                tiles, kept, sent, turned, sems):
    core = core_ref[0]
    group = K_MAX // 4

    def fetch(g):
        slots = pl.ds(g * group, group)
        return pltpu.make_async_copy(tiles_hbm.at[tick, slots], tiles.at[slots], sems.at[g])

    def put(g, which):
        buf, hbm = ((kept, kept_hbm), (sent, sent_hbm))[which]
        slots = pl.ds(g * group, group)
        return pltpu.make_async_copy(buf.at[slots], hbm.at[slots], sems.at[4 + 2 * g + which])

    for g in range(4):
        fetch(g).start()
    lane = lax.broadcasted_iota(jnp.int32, (8, TILE), 1)
    row = jnp.full((8, TILE), -1, jnp.int32)
    for k in range(K_MAX):
        cell = rows_ref[tick, k] * I_TILES + cols_ref[tick, k]
        row = jnp.where((lane == cell) & (k < count_ref[tick, 0]), k, row)
    sent[K_MAX, pl.ds(0, 8), :] = row.astype(f32)
    sent[K_MAX, pl.ds(8, HALF - 8), :] = jnp.zeros((HALF - 8, TILE), f32)
    last = pltpu.make_async_copy(sent.at[pl.ds(K_MAX, 1)], sent_hbm.at[pl.ds(K_MAX, 1)], sems.at[12])
    last.start()
    for g in range(4):
        fetch(g).wait()
        for k in range(g * group, (g + 1) * group):
            turned[k] = tiles[k].T
            for part in range(2):
                rows = pl.ds(part * SHARE, SHARE)
                mine = pl.multiple_of(part * HALF + core * SHARE, SHARE)
                theirs = pl.multiple_of(part * HALF + (1 - core) * SHARE, SHARE)
                kept[k, rows, :] = turned[k, pl.ds(mine, SHARE), :].astype(f32)
                sent[k, rows, :] = turned[k, pl.ds(theirs, SHARE), :].astype(f32)
        put(g, 0).start()
        put(g, 1).start()
    for g in range(4):
        put(g, 0).wait()
        put(g, 1).wait()
    last.wait()


def turned_tiles(tick, core, rows, cols, count, ratings):
    tile = pltpu.VMEM((K_MAX, TILE, TILE), bf16)
    return call(
        functools.partial(turn_kernel, tick),
        (shape((K_MAX, HALF, TILE), f32), shape((K_MAX + 1, HALF, TILE), f32)),
        [SMEM] * 4 + [ANY], (ANY, ANY),
        [tile, pltpu.VMEM((K_MAX, HALF, TILE), f32), pltpu.VMEM((K_MAX + 1, HALF, TILE), f32), tile,
         pltpu.SemaphoreType.DMA((13,))],
        1000000, 1600000,
    )(core, rows, cols, count, ratings)


def step_kernel(tick, last, rows_ref, cols_ref, count_ref, other_map, panel_hbm, own_users, other_users, own_hbm, other_hbm, *refs):
    item_hbm, *user_hbm = refs[:3] if last else refs[:2]
    panel_ref, users, own_tiles, other_tiles, predicted, item_grad, user_grad, own_map, sems = refs[-9:]
    half = BLOCKS // 2
    parts = ITEMS_CORE // TILE

    def rows(block):
        return pl.ds(block * WIDTH, WIDTH)

    panel_load = pltpu.make_async_copy(panel_hbm, panel_ref, sems.at[0])
    own_load = pltpu.make_async_copy(own_hbm, own_tiles, sems.at[1])
    other_load = pltpu.make_async_copy(other_hbm.at[pl.ds(0, K_MAX)], other_tiles, sems.at[2])
    user_loads = [
        pltpu.make_async_copy(
            (own_users if block < half else other_users).at[rows(block % half)], users.at[rows(block)],
            sems.at[3 + block])
        for block in range(BLOCKS)
    ]

    def send_items(part):
        cut = pl.ds(part * TILE, TILE)
        return pltpu.make_async_copy(item_grad.at[cut], item_hbm.at[cut], sems.at[3 + BLOCKS + part])

    def send_users(block):
        into = user_hbm[block // half].at[rows(block % half)] if last else user_hbm[0].at[rows(block)]
        return pltpu.make_async_copy(user_grad.at[rows(block)], into, sems.at[3 + BLOCKS + parts + block])

    for copy in [panel_load, *user_loads[:2], own_load, *user_loads[2:], other_load]:
        copy.start()
    for cell in range(CELLS):
        own_map[cell] = -1
    for k in range(K_MAX):
        cell = rows_ref[tick, k] * I_TILES + cols_ref[tick, k]
        own_map[cell] = jnp.where(k < count_ref[tick, 0], k, own_map[cell])

    def split(block):
        return halves(users[rows(block), :])

    def predict(block):
        predicted[block] = dot3(panel, split(block), ((1,), (1,)))

    def errors(block):
        tiles = own_tiles if block < half else other_tiles
        tops, lows = [], []
        for item in range(I_TILES):
            cut = pl.ds(item * HALF, HALF)
            cells = []
            for part in range(2):
                place = (block * 2 + part) % U_TILES * I_TILES + item
                slot = (own_map if block < half else other_map)[place]
                cell = tiles[jnp.maximum(slot, 0)] - predicted[block, cut, pl.ds(part * TILE, TILE)]
                cells.append(jnp.where(slot >= 0, cell, 0.0))
            top, low = halves(jnp.concatenate(cells, axis=1))
            tops.append(top)
            lows.append(low)
        return jnp.concatenate(tops, axis=0), jnp.concatenate(lows, axis=0)

    def user_part(block, error):
        user_grad[rows(block), :] = dot3(error, panel, ((0,), (0,)))

    def item_part(block, error):
        grad = dot3(error, split(block), ((1,), (0,)))
        if block == 0:
            item_grad[...] = grad
        else:
            item_grad[...] += grad

    panel_load.wait()
    user_loads[0].wait()
    user_loads[1].wait()
    panel = halves(panel_ref[...])
    predict(0)
    predict(1)
    own_load.wait()
    user_loads[2].wait()
    user_loads[3].wait()
    other_load.wait()
    error = errors(0)
    predict(2)
    item_part(0, error)
    user_part(0, error)
    error = errors(1)
    predict(3)
    item_part(1, error)
    user_part(1, error)
    send_users(0).start()
    send_users(1).start()
    error = errors(2)
    later = errors(3)
    user_part(2, error)
    item_part(2, error)
    item_part(3, later)
    for part in range(parts):
        send_items(part).start()
    send_users(2).start()
    user_part(3, later)
    send_users(3).start()
    for block in range(BLOCKS):
        send_users(block).wait()
    for part in range(parts):
        send_items(part).wait()


def item_and_user_grads(tick, last, rows, cols, count, other_map, panel, own, other, own_tiles, other_tiles):
    half_panel = pltpu.VMEM((ITEMS_CORE, R), f32)
    both = pltpu.VMEM((2 * U_DEV, R), f32)
    cut = (K_MAX, HALF, TILE)
    users = [shape((U_DEV, R), f32)] * 2 if last else [shape((2 * U_DEV, R), f32)]
    return call(
        functools.partial(step_kernel, tick, last),
        (shape((ITEMS_CORE, R), f32), *users),
        [SMEM] * 4 + [ANY] * 5, (ANY,) * (1 + len(users)),
        [half_panel, both, pltpu.VMEM(cut, f32), pltpu.VMEM(cut, f32),
         pltpu.VMEM((BLOCKS, ITEMS_CORE, WIDTH), f32), half_panel, both, pltpu.SMEM((CELLS,), jnp.int32),
         pltpu.SemaphoreType.DMA((3 + 2 * BLOCKS + ITEMS_CORE // TILE,))],
        2400000000, 4000000, STEP_GRANT,
    )(rows, cols, count, other_map, panel, own, other, own_tiles, other_tiles)


def stepped(user, here, there):
    return user * (1.0 - user_rate * shrink_rate) + user_rate * (here + there)


def update_kernel(own_hbm, other_hbm, here_hbm, there_hbm, own_out, other_out, user, here, there, sems):
    half = BLOCKS // 2

    def rows(block):
        return pl.ds(block * WIDTH, WIDTH)

    def part(block, own, other):
        return (own if block < half else other).at[rows(block % half)]

    def fetch(block, which):
        source, into = (
            (part(block, own_hbm, other_hbm), user),
            (here_hbm.at[rows(block)], here),
            (there_hbm.at[rows((block + half) % BLOCKS)], there),
        )[which]
        return pltpu.make_async_copy(source, into.at[rows(block)], sems.at[4 * block + which])

    def put(block):
        return pltpu.make_async_copy(user.at[rows(block)], part(block, own_out, other_out), sems.at[4 * block + 3])

    for block in range(BLOCKS):
        for which in range(3):
            fetch(block, which).start()
    for block in range(BLOCKS):
        for which in range(3):
            fetch(block, which).wait()
        user[rows(block), :] = stepped(user[rows(block), :], here[rows(block), :], there[rows(block), :])
        put(block).start()
    for block in range(BLOCKS):
        put(block).wait()


def updated_users(own, other, here, there):
    new = shape((U_DEV, R), f32)
    both = pltpu.VMEM((2 * U_DEV, R), f32)
    return call(
        update_kernel, (new, new), [ANY] * 4, (ANY, ANY),
        [both, both, both, pltpu.SemaphoreType.DMA((4 * BLOCKS,))], 1000000, 4000000, UPDATE_GRANT,
    )(own, other, here, there)


def swapped(x):
    return lax.ppermute(x, "owner", PARTNERS)


def exchanged(blocks):
    return lax.all_to_all(blocks, "owner", split_axis=0, concat_axis=0, axis_index_groups=SAME_CORE, tiled=True)


def passed_along(block, axis, distance):
    devices = range(lax.axis_size(axis))
    route = [((i - distance) % len(devices), i) for i in devices]
    return lax.ppermute(block, axis, route)


def shards(user_factors, item_factors, ratings, tile_users, tile_items, tile_count):
    core = lax.rem(lax.axis_index("owner"), 2).reshape(1)
    own, share = user_factors, item_factors
    other = swapped(own)
    for tick in range(TICKS):
        kept, sent = turned_tiles(tick, core, tile_users, tile_items, tile_count, ratings)
        got = swapped(sent)
        if tick == 0:
            got, other = lax.optimization_barrier((got, other))
        other_map = got[K_MAX, 0, :CELLS].astype(jnp.int32)
        panel = exchanged(jnp.broadcast_to(share[None], (CHIPS, SHARE, R))).reshape(ITEMS_CORE, R)
        item_grad, *here = item_and_user_grads(
            tick, tick + 1 == TICKS, tile_users, tile_items, tile_count, other_map, panel, own, other, kept, got)
        parts = exchanged(item_grad.reshape(CHIPS, SHARE, R))
        if tick + 1 < TICKS:
            there = swapped(here[0])
        else:
            there = swapped(here[1])
            own, parts = lax.optimization_barrier((stepped(own, here[0], there), parts))
        share = share * (1.0 - item_rate * shrink_rate) + item_rate * parts.sum(axis=0)
        if tick + 1 < TICKS:
            share, there = lax.optimization_barrier((share, there))
            share = passed_along(share, "band", -1)
            own, other = updated_users(own, other, here[0], there)
    return own, share


def solution(mesh):
    placed = (
        P(("band", "owner"), None),
        P(("band", "owner"), None),
        P(None, ("band", "owner"), None, None),
        P(None, ("band", "owner")),
        P(None, ("band", "owner")),
        P(None, ("band", "owner")),
    )
    return jax.shard_map(
        shards,
        mesh=mesh,
        in_specs=placed,
        out_specs=(P(("band", "owner"), None), P(("band", "owner"), None)),
        check_vma=False,
    )
```

```python
import functools

import jax
import jax.numpy as jnp
from jax import lax
from jax.experimental import pallas as pl
from jax.experimental.pallas import tpu as pltpu
from jax.sharding import PartitionSpec as P

R = 256
P_SIZE = 1024
TILE = 128
HALF = TILE // 2
TICKS = 3
K_MAX = 16
U_DEV = 512
U_TILES = U_DEV // TILE
I_TILES = P_SIZE // TILE
ITEMS_CORE = P_SIZE // 2
CHIPS = 16
SHARE = 32
CELLS = U_TILES * I_TILES

user_rate = 0.02
item_rate = 0.005
shrink_rate = 0.05
bf16 = jnp.bfloat16
f32 = jnp.float32

SAME_CORE = [[2 * chip + core for chip in range(CHIPS)] for core in range(2)]
PARTNERS = [(i, i ^ 1) for i in range(2 * CHIPS)]


def halves(x):
    top = x.astype(bf16)
    return top, (x - top.astype(f32)).astype(bf16)


def dot3(a, b, dims):
    (a_top, a_low), (b_top, b_low) = a, b
    dot = lambda x, y: lax.dot_general(x, y, (dims, ((), ())), preferred_element_type=f32)
    return dot(a_top, b_top) + (dot(a_top, b_low) + dot(a_low, b_top))


VMEM = pl.BlockSpec(memory_space=pltpu.VMEM)
ANY = pl.BlockSpec(memory_space=pl.ANY)
SMEM = pl.BlockSpec(memory_space=pltpu.SMEM)
WIDTH = 2 * TILE
BLOCKS = 2 * U_DEV // WIDTH
FIRST_GRANT = 53000
STEP_GRANT = 54000
LAST_GRANT = 53000
UPDATE_GRANT = 60 * 1024


def shape(dims, dtype):
    return jax.ShapeDtypeStruct(dims, dtype)


def call(kernel, outs, in_specs, out_specs, scratch, flops, nbytes, grant=60 * 1024):
    return pl.pallas_call(
        kernel,
        out_shape=outs,
        in_specs=in_specs,
        out_specs=out_specs,
        scratch_shapes=scratch,
        compiler_params=pltpu.CompilerParams(vmem_limit_bytes=grant * 1024),
        cost_estimate=pl.CostEstimate(flops=flops, bytes_accessed=nbytes, transcendentals=0),
    )


def turn_kernel(tick, core_ref, rows_ref, cols_ref, count_ref, tiles_hbm, kept_hbm, sent_hbm,
                tiles, kept, sent, turned, sems):
    core = core_ref[0]
    group = K_MAX // 4

    def fetch(g):
        slots = pl.ds(g * group, group)
        return pltpu.make_async_copy(tiles_hbm.at[tick, slots], tiles.at[slots], sems.at[g])

    def put(g, which):
        buf, hbm = ((kept, kept_hbm), (sent, sent_hbm))[which]
        slots = pl.ds(g * group, group)
        return pltpu.make_async_copy(buf.at[slots], hbm.at[slots], sems.at[4 + 2 * g + which])

    for g in range(4):
        fetch(g).start()
    lane = lax.broadcasted_iota(jnp.int32, (8, TILE), 1)
    row = jnp.full((8, TILE), -1, jnp.int32)
    for k in range(K_MAX):
        cell = rows_ref[tick, k] * I_TILES + cols_ref[tick, k]
        row = jnp.where((lane == cell) & (k < count_ref[tick]), k, row)
    sent[K_MAX, pl.ds(0, 8), :] = row.astype(f32)
    sent[K_MAX, pl.ds(8, HALF - 8), :] = jnp.zeros((HALF - 8, TILE), f32)
    last = pltpu.make_async_copy(sent.at[pl.ds(K_MAX, 1)], sent_hbm.at[pl.ds(K_MAX, 1)], sems.at[12])
    last.start()
    for g in range(4):
        fetch(g).wait()
        for k in range(g * group, (g + 1) * group):
            turned[k] = tiles[k].T
            for part in range(2):
                rows = pl.ds(part * SHARE, SHARE)
                mine = pl.multiple_of(part * HALF + core * SHARE, SHARE)
                theirs = pl.multiple_of(part * HALF + (1 - core) * SHARE, SHARE)
                kept[k, rows, :] = turned[k, pl.ds(mine, SHARE), :].astype(f32)
                sent[k, rows, :] = turned[k, pl.ds(theirs, SHARE), :].astype(f32)
        put(g, 0).start()
        put(g, 1).start()
    for g in range(4):
        put(g, 0).wait()
        put(g, 1).wait()
    last.wait()


def turned_tiles(tick, core, rows, cols, count, ratings):
    tile = pltpu.VMEM((K_MAX, TILE, TILE), bf16)
    return call(
        functools.partial(turn_kernel, tick),
        (shape((K_MAX, HALF, TILE), f32), shape((K_MAX + 1, HALF, TILE), f32)),
        [SMEM] * 4 + [ANY], (ANY, ANY),
        [tile, pltpu.VMEM((K_MAX, HALF, TILE), f32), pltpu.VMEM((K_MAX + 1, HALF, TILE), f32), tile,
         pltpu.SemaphoreType.DMA((13,))],
        1000000, 1600000,
    )(core, rows, cols, count, ratings)


def step_kernel(tick, last, rows_ref, cols_ref, count_ref, other_map, panel_hbm, own_users, other_users, own_hbm, other_hbm, *refs):
    item_hbm, *user_hbm = refs[:3] if last else refs[:2]
    panel_ref, users, own_tiles, other_tiles, predicted, item_grad, user_grad, own_map, sems = refs[-9:]
    half = BLOCKS // 2
    parts = ITEMS_CORE // TILE

    def rows(block):
        return pl.ds(block * WIDTH, WIDTH)

    panel_load = pltpu.make_async_copy(panel_hbm, panel_ref, sems.at[0])
    own_load = pltpu.make_async_copy(own_hbm, own_tiles, sems.at[1])
    other_load = pltpu.make_async_copy(other_hbm.at[pl.ds(0, K_MAX)], other_tiles, sems.at[2])
    user_loads = [
        pltpu.make_async_copy(
            (own_users if block < half else other_users).at[rows(block % half)], users.at[rows(block)],
            sems.at[3 + block])
        for block in range(BLOCKS)
    ]

    def send_items(part):
        cut = pl.ds(part * TILE, TILE)
        return pltpu.make_async_copy(item_grad.at[cut], item_hbm.at[cut], sems.at[3 + BLOCKS + part])

    def send_users(block):
        into = user_hbm[block // half].at[rows(block % half)] if last else user_hbm[0].at[rows(block)]
        return pltpu.make_async_copy(user_grad.at[rows(block)], into, sems.at[3 + BLOCKS + parts + block])

    for copy in [panel_load, *user_loads[:2], own_load, *user_loads[2:], other_load]:
        copy.start()
    for cell in range(CELLS):
        own_map[cell] = -1
    for k in range(K_MAX):
        cell = rows_ref[tick, k] * I_TILES + cols_ref[tick, k]
        own_map[cell] = jnp.where(k < count_ref[tick], k, own_map[cell])

    def split(block):
        return halves(users[rows(block), :])

    def predict(block):
        predicted[block] = dot3(panel, split(block), ((1,), (1,)))

    def errors(block):
        tiles = own_tiles if block < half else other_tiles
        tops, lows = [], []
        for item in range(I_TILES):
            cut = pl.ds(item * HALF, HALF)
            cells = []
            for part in range(2):
                place = (block * 2 + part) % U_TILES * I_TILES + item
                slot = (own_map if block < half else other_map)[place]
                cell = tiles[jnp.maximum(slot, 0)] - predicted[block, cut, pl.ds(part * TILE, TILE)]
                cells.append(jnp.where(slot >= 0, cell, 0.0))
            top, low = halves(jnp.concatenate(cells, axis=1))
            tops.append(top)
            lows.append(low)
        return jnp.concatenate(tops, axis=0), jnp.concatenate(lows, axis=0)

    def user_part(block, error):
        user_grad[rows(block), :] = dot3(error, panel, ((0,), (0,)))

    def item_part(block, error):
        grad = dot3(error, split(block), ((1,), (0,)))
        if block == 0:
            item_grad[...] = grad
        else:
            item_grad[...] += grad

    panel_load.wait()
    panel = halves(panel_ref[...])
    user_loads[0].wait()
    user_loads[1].wait()
    predict(0)
    predict(1)
    own_load.wait()
    user_loads[2].wait()
    user_loads[3].wait()
    other_load.wait()
    error = errors(0)
    predict(2)
    item_part(0, error)
    user_part(0, error)
    error = errors(1)
    predict(3)
    item_part(1, error)
    user_part(1, error)
    send_users(0).start()
    send_users(1).start()
    error = errors(2)
    later = errors(3)
    user_part(2, error)
    item_part(2, error)
    item_part(3, later)
    for part in range(parts):
        send_items(part).start()
    send_users(2).start()
    user_part(3, later)
    send_users(3).start()
    for block in range(BLOCKS):
        send_users(block).wait()
    for part in range(parts):
        send_items(part).wait()


def item_and_user_grads(tick, last, rows, cols, count, other_map, panel, own, other, own_tiles, other_tiles):
    half_panel = pltpu.VMEM((ITEMS_CORE, R), f32)
    both = pltpu.VMEM((2 * U_DEV, R), f32)
    cut = (K_MAX, HALF, TILE)
    users = [shape((U_DEV, R), f32)] * 2 if last else [shape((2 * U_DEV, R), f32)]
    return call(
        functools.partial(step_kernel, tick, last),
        (shape((ITEMS_CORE, R), f32), *users),
        [SMEM] * 4 + [ANY] * 5, (ANY,) * (1 + len(users)),
        [half_panel, both, pltpu.VMEM(cut, f32), pltpu.VMEM(cut, f32),
         pltpu.VMEM((BLOCKS, ITEMS_CORE, WIDTH), f32), half_panel, both, pltpu.SMEM((CELLS,), jnp.int32),
         pltpu.SemaphoreType.DMA((3 + 2 * BLOCKS + ITEMS_CORE // TILE,))],
        2400000000, 4000000, (FIRST_GRANT, STEP_GRANT, LAST_GRANT)[tick],
    )(rows, cols, count, other_map, panel, own, other, own_tiles, other_tiles)


def stepped(user, here, there):
    return user * (1.0 - user_rate * shrink_rate) + user_rate * (here + there)


def update_kernel(own_hbm, other_hbm, here_hbm, there_hbm, own_out, other_out, user, here, there, sems):
    half = BLOCKS // 2

    def rows(block):
        return pl.ds(block * WIDTH, WIDTH)

    def part(block, own, other):
        return (own if block < half else other).at[rows(block % half)]

    def fetch(block, which):
        source, into = (
            (part(block, own_hbm, other_hbm), user),
            (here_hbm.at[rows(block)], here),
            (there_hbm.at[rows((block + half) % BLOCKS)], there),
        )[which]
        return pltpu.make_async_copy(source, into.at[rows(block)], sems.at[4 * block + which])

    def put(block):
        return pltpu.make_async_copy(user.at[rows(block)], part(block, own_out, other_out), sems.at[4 * block + 3])

    for block in range(BLOCKS):
        for which in range(3):
            fetch(block, which).start()
    for block in range(BLOCKS):
        for which in range(3):
            fetch(block, which).wait()
        user[rows(block), :] = stepped(user[rows(block), :], here[rows(block), :], there[rows(block), :])
        put(block).start()
    for block in range(BLOCKS):
        put(block).wait()


def updated_users(own, other, here, there):
    new = shape((U_DEV, R), f32)
    both = pltpu.VMEM((2 * U_DEV, R), f32)
    return call(
        update_kernel, (new, new), [ANY] * 4, (ANY, ANY),
        [both, both, both, pltpu.SemaphoreType.DMA((4 * BLOCKS,))], 1000000, 4000000, UPDATE_GRANT,
    )(own, other, here, there)


def swapped(x):
    return lax.ppermute(x, "owner", PARTNERS)


def exchanged(blocks):
    return lax.all_to_all(blocks, "owner", split_axis=0, concat_axis=0, axis_index_groups=SAME_CORE, tiled=True)


def passed_along(block, axis, distance):
    devices = range(lax.axis_size(axis))
    route = [((i - distance) % len(devices), i) for i in devices]
    return lax.ppermute(block, axis, route)


def shards(user_factors, item_factors, ratings, tile_users, tile_items, tile_count):
    core = lax.rem(lax.axis_index("owner"), 2).reshape(1)
    own, share = user_factors, item_factors
    tile_count = tile_count.reshape(TICKS)
    other = swapped(own)
    for tick in range(TICKS):
        kept, sent = turned_tiles(tick, core, tile_users, tile_items, tile_count, ratings)
        got = swapped(sent)
        if tick == 0:
            got, other = lax.optimization_barrier((got, other))
        other_map = got[K_MAX, 0, :CELLS].astype(jnp.int32)
        panel = exchanged(jnp.broadcast_to(share[None], (CHIPS, SHARE, R))).reshape(ITEMS_CORE, R)
        item_grad, *here = item_and_user_grads(
            tick, tick + 1 == TICKS, tile_users, tile_items, tile_count, other_map, panel, own, other, kept, got)
        parts = exchanged(item_grad.reshape(CHIPS, SHARE, R))
        if tick + 1 < TICKS:
            there = swapped(here[0])
        else:
            there = swapped(here[1])
            own, parts = lax.optimization_barrier((stepped(own, here[0], there), parts))
        share = share * (1.0 - item_rate * shrink_rate) + item_rate * parts.sum(axis=0)
        if tick + 1 < TICKS:
            share, there = lax.optimization_barrier((share, there))
            share = passed_along(share, "band", -1)
            own, other = updated_users(own, other, here[0], there)
    return own, share


def solution(mesh):
    placed = (
        P(("band", "owner"), None),
        P(("band", "owner"), None),
        P(None, ("band", "owner"), None, None),
        P(None, ("band", "owner")),
        P(None, ("band", "owner")),
        P(None, ("band", "owner")),
    )
    return jax.shard_map(
        shards,
        mesh=mesh,
        in_specs=placed,
        out_specs=(P(("band", "owner"), None), P(("band", "owner"), None)),
        check_vma=False,
    )
```

```python
import functools

import jax
import jax.numpy as jnp
from jax import lax
from jax.experimental import pallas as pl
from jax.experimental.pallas import tpu as pltpu
from jax.sharding import PartitionSpec as P

R = 256
P_SIZE = 1024
TILE = 128
HALF = TILE // 2
TICKS = 3
K_MAX = 16
U_DEV = 512
U_TILES = U_DEV // TILE
I_TILES = P_SIZE // TILE
ITEMS_CORE = P_SIZE // 2
CHIPS = 16
SHARE = 32
CELLS = U_TILES * I_TILES

user_rate = 0.02
item_rate = 0.005
shrink_rate = 0.05
bf16 = jnp.bfloat16
f32 = jnp.float32

SAME_CORE = [[2 * chip + core for chip in range(CHIPS)] for core in range(2)]
PARTNERS = [(i, i ^ 1) for i in range(2 * CHIPS)]


def halves(x):
    top = x.astype(bf16)
    return top, (x - top.astype(f32)).astype(bf16)


def dot3(a, b, dims):
    (a_top, a_low), (b_top, b_low) = a, b
    dot = lambda x, y: lax.dot_general(x, y, (dims, ((), ())), preferred_element_type=f32)
    return dot(a_top, b_top) + (dot(a_top, b_low) + dot(a_low, b_top))


VMEM = pl.BlockSpec(memory_space=pltpu.VMEM)
ANY = pl.BlockSpec(memory_space=pl.ANY)
SMEM = pl.BlockSpec(memory_space=pltpu.SMEM)
WIDTH = 2 * TILE
BLOCKS = 2 * U_DEV // WIDTH
FIRST_GRANT = 53000
STEP_GRANT = 54000
LAST_GRANT = 53000
UPDATE_GRANT = 60 * 1024


def shape(dims, dtype):
    return jax.ShapeDtypeStruct(dims, dtype)


def call(kernel, outs, in_specs, out_specs, scratch, flops, nbytes, grant=60 * 1024):
    return pl.pallas_call(
        kernel,
        out_shape=outs,
        in_specs=in_specs,
        out_specs=out_specs,
        scratch_shapes=scratch,
        compiler_params=pltpu.CompilerParams(vmem_limit_bytes=grant * 1024),
        cost_estimate=pl.CostEstimate(flops=flops, bytes_accessed=nbytes, transcendentals=0),
    )


def turn_kernel(ticks, core_ref, rows_ref, cols_ref, count_ref, tiles_hbm, kept_hbm, sent_hbm,
                tiles, kept, sent, turned, sems):
    core = core_ref[0]
    group = K_MAX // 4
    groups = [(j, tick, g) for j, tick in enumerate(ticks) for g in range(4)]

    def fetch(j, tick, g):
        return pltpu.make_async_copy(
            tiles_hbm.at[tick, pl.ds(g * group, group)], tiles.at[pl.ds(j * K_MAX + g * group, group)],
            sems.at[13 * j + g])

    def put(j, g, which):
        buf, hbm, stride = ((kept, kept_hbm, K_MAX), (sent, sent_hbm, K_MAX + 1))[which]
        slots = pl.ds(j * stride + g * group, group)
        return pltpu.make_async_copy(buf.at[slots], hbm.at[slots], sems.at[13 * j + 4 + 2 * g + which])

    def put_map(j):
        slot = pl.ds(j * (K_MAX + 1) + K_MAX, 1)
        return pltpu.make_async_copy(sent.at[slot], sent_hbm.at[slot], sems.at[13 * j + 12])

    for at in groups:
        fetch(*at).start()
    lane = lax.broadcasted_iota(jnp.int32, (8, TILE), 1)
    for j, tick in enumerate(ticks):
        row = jnp.full((8, TILE), -1, jnp.int32)
        for k in range(K_MAX):
            cell = rows_ref[tick, k] * I_TILES + cols_ref[tick, k]
            row = jnp.where((lane == cell) & (k < count_ref[tick]), k, row)
        sent[j * (K_MAX + 1) + K_MAX, pl.ds(0, 8), :] = row.astype(f32)
        sent[j * (K_MAX + 1) + K_MAX, pl.ds(8, HALF - 8), :] = jnp.zeros((HALF - 8, TILE), f32)
        put_map(j).start()
    for j, tick, g in groups:
        fetch(j, tick, g).wait()
        for k in range(g * group, (g + 1) * group):
            at = j * K_MAX + k
            turned[at] = tiles[at].T
            for part in range(2):
                rows = pl.ds(part * SHARE, SHARE)
                mine = pl.multiple_of(part * HALF + core * SHARE, SHARE)
                theirs = pl.multiple_of(part * HALF + (1 - core) * SHARE, SHARE)
                kept[at, rows, :] = turned[at, pl.ds(mine, SHARE), :].astype(f32)
                sent[at + j, rows, :] = turned[at, pl.ds(theirs, SHARE), :].astype(f32)
        put(j, g, 0).start()
        put(j, g, 1).start()
    for j, tick, g in groups:
        put(j, g, 0).wait()
        put(j, g, 1).wait()
    for j in range(len(ticks)):
        put_map(j).wait()


def turned_tiles(ticks, core, rows, cols, count, ratings):
    n = len(ticks)
    kept, sent = (n * K_MAX, HALF, TILE), (n * (K_MAX + 1), HALF, TILE)
    tile = pltpu.VMEM((n * K_MAX, TILE, TILE), bf16)
    return call(
        functools.partial(turn_kernel, ticks),
        (shape(kept, f32), shape(sent, f32)),
        [SMEM] * 4 + [ANY], (ANY, ANY),
        [tile, pltpu.VMEM(kept, f32), pltpu.VMEM(sent, f32), tile, pltpu.SemaphoreType.DMA((13 * n,))],
        1000000, 1600000 * n,
    )(core, rows, cols, count, ratings)


def step_kernel(tick, last, rows_ref, cols_ref, count_ref, other_map, panel_hbm, own_users, other_users, own_hbm, other_hbm, *refs):
    item_hbm, *user_hbm = refs[:3] if last else refs[:2]
    panel_ref, users, own_tiles, other_tiles, predicted, item_grad, user_grad, own_map, sems = refs[-9:]
    half = BLOCKS // 2
    parts = ITEMS_CORE // TILE
    part_of = max(tick - 1, 0)

    def rows(block):
        return pl.ds(block * WIDTH, WIDTH)

    panel_load = pltpu.make_async_copy(panel_hbm, panel_ref, sems.at[0])
    own_load = pltpu.make_async_copy(own_hbm.at[pl.ds(part_of * K_MAX, K_MAX)], own_tiles, sems.at[1])
    other_load = pltpu.make_async_copy(
        other_hbm.at[pl.ds(part_of * (K_MAX + 1), K_MAX)], other_tiles, sems.at[2])
    user_loads = [
        pltpu.make_async_copy(
            (own_users if block < half else other_users).at[rows(block % half)], users.at[rows(block)],
            sems.at[3 + block])
        for block in range(BLOCKS)
    ]

    def send_items(part):
        cut = pl.ds(part * TILE, TILE)
        return pltpu.make_async_copy(item_grad.at[cut], item_hbm.at[cut], sems.at[3 + BLOCKS + part])

    def send_users(block):
        into = user_hbm[block // half].at[rows(block % half)] if last else user_hbm[0].at[rows(block)]
        return pltpu.make_async_copy(user_grad.at[rows(block)], into, sems.at[3 + BLOCKS + parts + block])

    for copy in [panel_load, *user_loads[:2], own_load, *user_loads[2:], other_load]:
        copy.start()
    for cell in range(CELLS):
        own_map[cell] = -1
    for k in range(K_MAX):
        cell = rows_ref[tick, k] * I_TILES + cols_ref[tick, k]
        own_map[cell] = jnp.where(k < count_ref[tick], k, own_map[cell])

    def split(block):
        return halves(users[rows(block), :])

    def predict(block):
        predicted[block] = dot3(panel, split(block), ((1,), (1,)))

    def errors(block):
        tiles = own_tiles if block < half else other_tiles
        tops, lows = [], []
        for item in range(I_TILES):
            cut = pl.ds(item * HALF, HALF)
            cells = []
            for part in range(2):
                place = (block * 2 + part) % U_TILES * I_TILES + item
                slot = (own_map if block < half else other_map)[place]
                cell = tiles[jnp.maximum(slot, 0)] - predicted[block, cut, pl.ds(part * TILE, TILE)]
                cells.append(jnp.where(slot >= 0, cell, 0.0))
            top, low = halves(jnp.concatenate(cells, axis=1))
            tops.append(top)
            lows.append(low)
        return jnp.concatenate(tops, axis=0), jnp.concatenate(lows, axis=0)

    def user_part(block, error):
        user_grad[rows(block), :] = dot3(error, panel, ((0,), (0,)))

    def item_part(block, error):
        grad = dot3(error, split(block), ((1,), (0,)))
        if block == 0:
            item_grad[...] = grad
        else:
            item_grad[...] += grad

    panel_load.wait()
    panel = halves(panel_ref[...])
    user_loads[0].wait()
    user_loads[1].wait()
    predict(0)
    predict(1)
    own_load.wait()
    user_loads[2].wait()
    user_loads[3].wait()
    other_load.wait()
    error = errors(0)
    predict(2)
    item_part(0, error)
    user_part(0, error)
    error = errors(1)
    predict(3)
    item_part(1, error)
    user_part(1, error)
    send_users(0).start()
    send_users(1).start()
    error = errors(2)
    later = errors(3)
    user_part(2, error)
    item_part(2, error)
    item_part(3, later)
    for part in range(parts):
        send_items(part).start()
    send_users(2).start()
    user_part(3, later)
    send_users(3).start()
    for block in range(BLOCKS):
        send_users(block).wait()
    for part in range(parts):
        send_items(part).wait()


def item_and_user_grads(tick, last, rows, cols, count, other_map, panel, own, other, own_tiles, other_tiles):
    half_panel = pltpu.VMEM((ITEMS_CORE, R), f32)
    both = pltpu.VMEM((2 * U_DEV, R), f32)
    cut = (K_MAX, HALF, TILE)
    users = [shape((U_DEV, R), f32)] * 2 if last else [shape((2 * U_DEV, R), f32)]
    return call(
        functools.partial(step_kernel, tick, last),
        (shape((ITEMS_CORE, R), f32), *users),
        [SMEM] * 4 + [ANY] * 5, (ANY,) * (1 + len(users)),
        [half_panel, both, pltpu.VMEM(cut, f32), pltpu.VMEM(cut, f32),
         pltpu.VMEM((BLOCKS, ITEMS_CORE, WIDTH), f32), half_panel, both, pltpu.SMEM((CELLS,), jnp.int32),
         pltpu.SemaphoreType.DMA((3 + 2 * BLOCKS + ITEMS_CORE // TILE,))],
        2400000000, 4000000, (FIRST_GRANT, STEP_GRANT, LAST_GRANT)[tick],
    )(rows, cols, count, other_map, panel, own, other, own_tiles, other_tiles)


def stepped(user, here, there):
    return user * (1.0 - user_rate * shrink_rate) + user_rate * (here + there)


def update_kernel(own_hbm, other_hbm, here_hbm, there_hbm, own_out, other_out, user, here, there, sems):
    half = BLOCKS // 2

    def rows(block):
        return pl.ds(block * WIDTH, WIDTH)

    def part(block, own, other):
        return (own if block < half else other).at[rows(block % half)]

    def fetch(block, which):
        source, into = (
            (part(block, own_hbm, other_hbm), user),
            (here_hbm.at[rows(block)], here),
            (there_hbm.at[rows((block + half) % BLOCKS)], there),
        )[which]
        return pltpu.make_async_copy(source, into.at[rows(block)], sems.at[4 * block + which])

    def put(block):
        return pltpu.make_async_copy(user.at[rows(block)], part(block, own_out, other_out), sems.at[4 * block + 3])

    for block in range(BLOCKS):
        for which in range(3):
            fetch(block, which).start()
    for block in range(BLOCKS):
        for which in range(3):
            fetch(block, which).wait()
        user[rows(block), :] = stepped(user[rows(block), :], here[rows(block), :], there[rows(block), :])
        put(block).start()
    for block in range(BLOCKS):
        put(block).wait()


def updated_users(own, other, here, there):
    new = shape((U_DEV, R), f32)
    both = pltpu.VMEM((2 * U_DEV, R), f32)
    return call(
        update_kernel, (new, new), [ANY] * 4, (ANY, ANY),
        [both, both, both, pltpu.SemaphoreType.DMA((4 * BLOCKS,))], 1000000, 4000000, UPDATE_GRANT,
    )(own, other, here, there)


def swapped(x):
    return lax.ppermute(x, "owner", PARTNERS)


def exchanged(blocks):
    return lax.all_to_all(blocks, "owner", split_axis=0, concat_axis=0, axis_index_groups=SAME_CORE, tiled=True)


def passed_along(block, axis, distance):
    devices = range(lax.axis_size(axis))
    route = [((i - distance) % len(devices), i) for i in devices]
    return lax.ppermute(block, axis, route)


def shards(user_factors, item_factors, ratings, tile_users, tile_items, tile_count):
    core = lax.rem(lax.axis_index("owner"), 2).reshape(1)
    own, share = user_factors, item_factors
    tile_count = tile_count.reshape(TICKS)
    other = swapped(own)
    for tick in range(TICKS):
        if tick < 2:
            kept, sent = turned_tiles(
                ((0,), (1, 2))[tick], core, tile_users, tile_items, tile_count, ratings)
            got = swapped(sent)
        if tick == 0:
            got, other = lax.optimization_barrier((got, other))
        other_map = got[max(tick - 1, 0) * (K_MAX + 1) + K_MAX, 0, :CELLS].astype(jnp.int32)
        panel = exchanged(jnp.broadcast_to(share[None], (CHIPS, SHARE, R))).reshape(ITEMS_CORE, R)
        item_grad, *here = item_and_user_grads(
            tick, tick + 1 == TICKS, tile_users, tile_items, tile_count, other_map, panel, own, other, kept, got)
        parts = exchanged(item_grad.reshape(CHIPS, SHARE, R))
        if tick + 1 < TICKS:
            there = swapped(here[0])
        else:
            there = swapped(here[1])
            own, parts = lax.optimization_barrier((stepped(own, here[0], there), parts))
        share = share * (1.0 - item_rate * shrink_rate) + item_rate * parts.sum(axis=0)
        if tick + 1 < TICKS:
            share, there = lax.optimization_barrier((share, there))
            share = passed_along(share, "band", -1)
            own, other = updated_users(own, other, here[0], there)
    return own, share


def solution(mesh):
    placed = (
        P(("band", "owner"), None),
        P(("band", "owner"), None),
        P(None, ("band", "owner"), None, None),
        P(None, ("band", "owner")),
        P(None, ("band", "owner")),
        P(None, ("band", "owner")),
    )
    return jax.shard_map(
        shards,
        mesh=mesh,
        in_specs=placed,
        out_specs=(P(("band", "owner"), None), P(("band", "owner"), None)),
        check_vma=False,
    )
```
